32 devices in a mesh: rows: 8 (over y, x, core), cols: 4 (over z).
Axes of the slice: x: 2, y: 2, z: 4, core: 2. Of those that a mesh axis runs over, the one named last changes fastest.
Arguments:
- grads: bfloat16 [9216, 8192], P(('rows', 'cols')), may hold values from -6 to 6
- tests: float32 [64, 8192], P(None, 'cols'), may hold values from -6 to 6
Outputs:
- solution: float32 [64, 8192], P(None, 'cols')
- scores: float32 [64, 9216], P(None, ('rows', 'cols'))
The draws below stay inside these ranges and needn't reach their ends.
All inputs are finite; a program needn't handle non-finite values.
Results may differ from the reference program's by a relative error of at most 0.0041.
Values may be sent and summed in bfloat16 or wider, within the bound.
A program may use at most 64 MiB of HBM per device.

```python
import jax
import jax.numpy as jnp
from jax import lax

K = 8192
TESTS = 64
ITERS = 2
N_TOTAL = 9216


def spiked(array, stream_key, source, target, blocks, factor):
    def block_of(dim):
        return (jnp.arange(array.shape[dim]) // (array.shape[dim] // blocks)).reshape((-1,) + (1,) * (array.ndim - 1 - dim))

    near = jax.random.permutation(stream_key, blocks)[block_of(target)]
    other_side = (block_of(target) + blocks // 2) % blocks
    return jnp.where((block_of(source) == near) | (block_of(source) == other_side), factor * array, array)


def level_of(rng, extent, cuts, low, largest):
    loudness, own = 1.0, jax.random.fold_in(rng, 6)
    for dim, blocks in cuts:
        heights = jnp.exp(jax.random.uniform(jax.random.fold_in(own, dim), (blocks,), jnp.float32, low / len(cuts), largest / len(cuts)))
        loudness = loudness * jnp.repeat(heights, extent[dim] // blocks).reshape([-1 if axis == dim else 1 for axis in range(len(extent))])
    return loudness


def centred(rng, extent, scale, most, shards=(), dtype=jnp.bfloat16):
    result = scale * jax.random.normal(rng, extent, jnp.float32)
    if shards:
        result = result * level_of(rng, extent, shards, -0.22, 0.18)
    return jnp.clip(result, -most, most).astype(dtype)


def noise_with(rng, extent, deviation, limit, split, heavy, held_as=jnp.bfloat16):
    array = deviation * jax.random.normal(rng, extent, jnp.float32)
    if split:
        array = array * level_of(rng, extent, split, -0.22, 0.18)
    return jnp.clip(spiked(array, jax.random.fold_in(rng, 3), *heavy), -limit, limit).astype(held_as)


def setup_inputs(seed: int = 0) -> dict:
    seeds = jax.random.split(jax.random.key(seed), 3)
    grads = noise_with(seeds[0], (N_TOTAL, K), 1.0, 6.0, ((0, 32),), (0, 1, 32, 2.75))
    tests = centred(seeds[1], (TESTS, K), 1.0, 6.0, ((1, 4),), jnp.float32)
    return {"grads": grads, "tests": tests}


damping = 0.5


def reference(grads, tests):
    n_total = grads.shape[0]
    width = grads.shape[1]
    solution = jnp.zeros(tests.shape, jnp.float32)
    residual = tests
    direction = tests
    norm_now = jnp.sum(residual * residual, axis=1)
    for step in range(ITERS):
        dir_bf = direction.astype(jnp.bfloat16)
        proj = lax.dot_general(grads, dir_bf, (((1,), (1,)), ((), ())), preferred_element_type=jnp.float32).astype(jnp.bfloat16)
        back = lax.dot_general(proj, grads, (((0,), (0,)), ((), ())), preferred_element_type=jnp.float32)
        image = back / n_total + damping * direction
        curv = jnp.sum(direction * image, axis=1)
        alpha = norm_now / curv
        solution = solution + alpha[:, None] * direction
        residual = residual - alpha[:, None] * image
        norm_next = jnp.sum(residual * residual, axis=1)
        direction = residual + (norm_next / norm_now)[:, None] * direction
        norm_now = norm_next
    sol_bf = solution.astype(jnp.bfloat16)
    scores = lax.dot_general(sol_bf, grads, (((1,), (1,)), ((), ())), preferred_element_type=jnp.float32)
    return solution, scores * (width ** -0.5)
```

```python
import jax
import jax.numpy as jnp
from jax import lax
from jax.sharding import PartitionSpec as P

damping = 0.5


def per_device(grads, tests):
    n_total = grads.shape[0] * lax.axis_size("rows") * lax.axis_size("cols")
    width = grads.shape[1]
    own = tests.shape[1]
    direction = lax.all_gather(tests, "cols", axis=1, tiled=True)
    norm_now = jnp.sum(direction * direction, axis=1)

    def project(d):
        return lax.dot_general(
            grads, d.astype(jnp.bfloat16), (((1,), (1,)), ((), ())), preferred_element_type=jnp.float32
        )

    partial_value = lax.dot_general(
        project(direction).astype(jnp.bfloat16), grads, (((0,), (0,)), ((), ())), preferred_element_type=jnp.float32
    )
    image = lax.psum(partial_value, ("rows", "cols")) / n_total + damping * direction
    alpha = norm_now / jnp.sum(direction * image, axis=1)
    solution = alpha[:, None] * direction
    residual = direction - alpha[:, None] * image
    norm_next = jnp.sum(residual * residual, axis=1)
    direction = residual + (norm_next / norm_now)[:, None] * direction
    proj = project(direction)
    curv = lax.psum(jnp.sum(proj * proj.astype(jnp.bfloat16).astype(jnp.float32), axis=0), ("rows", "cols"))
    curv = curv / n_total + damping * jnp.sum(direction * direction, axis=1)
    solution = solution + (norm_next / curv)[:, None] * direction
    scores = lax.dot_general(
        solution.astype(jnp.bfloat16), grads, (((1,), (1,)), ((), ())), preferred_element_type=jnp.float32
    )
    mine = lax.dynamic_slice_in_dim(solution, lax.axis_index("cols") * own, own, axis=1)
    return (mine, scores * width ** (-0.5))


def solution(mesh):
    placed = (P(("rows", "cols"), None), P(None, "cols"))
    return jax.shard_map(
        per_device,
        mesh=mesh,
        in_specs=placed,
        out_specs=(P(None, "cols"), P(None, ("rows", "cols"))),
        check_vma=False,
    )
```

```python
import functools

import jax
import jax.numpy as jnp
from jax import lax
from jax.experimental import pallas as pl
from jax.experimental.pallas import tpu as pltpu
from jax.sharding import PartitionSpec as P

MESH = pl.DeviceIdType.MESH
LANES = 2
BLOCK = 1024

damping = 0.5


def plain(grads, tests):
    n_total = grads.shape[0] * lax.axis_size("rows") * lax.axis_size("cols")
    width = grads.shape[1]
    own = tests.shape[1]
    direction = lax.all_gather(tests, "cols", axis=1, tiled=True)
    norm_now = jnp.sum(direction * direction, axis=1)

    def project(d):
        return lax.dot_general(
            grads, d.astype(jnp.bfloat16), (((1,), (1,)), ((), ())), preferred_element_type=jnp.float32
        )

    partial_value = lax.dot_general(
        project(direction).astype(jnp.bfloat16), grads, (((0,), (0,)), ((), ())), preferred_element_type=jnp.float32
    )
    image = lax.psum(partial_value, ("rows", "cols")) / n_total + damping * direction
    alpha = norm_now / jnp.sum(direction * image, axis=1)
    solution = alpha[:, None] * direction
    residual = direction - alpha[:, None] * image
    norm_next = jnp.sum(residual * residual, axis=1)
    direction = residual + (norm_next / norm_now)[:, None] * direction
    proj = project(direction)
    curv = lax.psum(jnp.sum(proj * proj.astype(jnp.bfloat16).astype(jnp.float32), axis=0), ("rows", "cols"))
    curv = curv / n_total + damping * jnp.sum(direction * direction, axis=1)
    solution = solution + (norm_next / curv)[:, None] * direction
    scores = lax.dot_general(
        solution.astype(jnp.bfloat16), grads, (((1,), (1,)), ((), ())), preferred_element_type=jnp.float32
    )
    mine = lax.dynamic_slice_in_dim(solution, lax.axis_index("cols") * own, own, axis=1)
    return (mine, scores * width ** (-0.5))


def bits_of(count):
    return count.bit_length() - 1


def reverse_bits(value, count):
    out = 0
    for _ in range(count):
        out, value = out * 2 + value % 2, value // 2
    return out


def kernel(nr, nc, grads, tests, out, scores, g, t, acc, img, box, mail, load_sem, own_sem, send_sem, recv_sem, csend, crecv):
    me = {"rows": lax.axis_index("rows"), "cols": lax.axis_index("cols")}
    n = nr * nc
    count, own = tests.shape
    width = grads.shape[1]
    chunk = width // n
    n_total = grads.shape[0] * n
    span = count // LANES
    rest = list(range(1, bits_of(nr)))
    low = [("cols", b) for b in range(bits_of(nc))]
    orders = [[("rows", b) for b in [0] + r] + low for r in (rest, rest[::-1])]
    stages = len(orders[0])

    def bit(stage):
        axis, b = stage
        return lax.rem(lax.div(me[axis], 2**b), 2)

    def partner(stage):
        axis, b = stage
        return {axis: me[axis] + (1 - 2 * bit(stage)) * 2**b}

    loads = []
    for v in range(n):
        at = reverse_bits(v % nc, bits_of(nc)) * nr + v // nc
        loads.append(
            pltpu.make_async_copy(
                grads.at[:, pl.ds(at * chunk, chunk)], g.at[:, pl.ds(v * chunk, chunk)], load_sem.at[v]
            )
        )
        loads[-1].start()

    rows = [pl.ds(lane * span, span) for lane in range(LANES)]
    place = []
    firsts = []
    for lane, order in enumerate(orders):
        v = 0
        for stage in order:
            v = v * 2 + bit(stage)
        place.append(v)
        copy = pltpu.make_async_copy(
            tests.at[rows[lane], pl.ds(pl.multiple_of(lax.div(v, nc) * chunk, chunk), chunk)],
            t.at[rows[lane], pl.ds(pl.multiple_of(v * chunk, chunk), chunk)],
            own_sem.at[lane],
        )
        copy.start()
        firsts.append(copy)

    barrier = pltpu.get_barrier_semaphore()
    for stage in orders[0]:
        pl.semaphore_signal(barrier, inc=1, device_id=partner(stage), device_id_type=MESH)
    pl.semaphore_wait(barrier, stages)

    def gather(buf, phase, ready):
        sent = []
        start = list(place)
        flying = [None] * LANES
        for k in range(stages):
            size = chunk * 2**k
            for lane in range(LANES):
                stage = orders[lane][stages - 1 - k]
                if k == 0:
                    ready(lane)
                else:
                    flying[lane].wait_recv()
                part = buf.at[rows[lane], pl.ds(pl.multiple_of(start[lane] * chunk, size), size)]
                flying[lane] = pltpu.make_async_remote_copy(
                    src_ref=part,
                    dst_ref=part,
                    send_sem=send_sem.at[phase, lane, k],
                    recv_sem=recv_sem.at[phase, lane, k],
                    device_id=partner(stage),
                    device_id_type=MESH,
                )
                flying[lane].start()
                sent.append(flying[lane])
                start[lane] = start[lane] - bit(stage) * 2**k
        for copy in flying:
            copy.wait_recv()
        return sent

    def scatter(phase):
        sent = []
        start = [0] * LANES
        flying = [None] * LANES
        offset = 0
        for k in range(stages + 1):
            half = width // 2 ** (k + 1)
            for lane in range(LANES):
                if k:
                    flying[lane].wait_recv()
                    at = pl.ds(pl.multiple_of(start[lane], 2 * half), 2 * half)
                    acc[rows[lane], at] = acc[rows[lane], at] + box[rows[lane], pl.ds(offset - 2 * half, 2 * half)]
                if k < stages:
                    stage = orders[lane][k]
                    give = start[lane] + (1 - bit(stage)) * half
                    start[lane] = start[lane] + bit(stage) * half
                    flying[lane] = pltpu.make_async_remote_copy(
                        src_ref=acc.at[rows[lane], pl.ds(pl.multiple_of(give, half), half)],
                        dst_ref=box.at[rows[lane], pl.ds(offset, half)],
                        send_sem=send_sem.at[phase, lane, k],
                        recv_sem=recv_sem.at[phase, lane, k],
                        device_id=partner(stage),
                        device_id_type=MESH,
                    )
                    flying[lane].start()
                    sent.append(flying[lane])
            offset += half
        return sent

    def fold(x):
        total = x[:, :128]
        for i in range(1, x.shape[1] // 128):
            total = total + x[:, i * 128 : (i + 1) * 128]
        return total

    def across(x):
        return jnp.sum(x, axis=1, keepdims=True)

    def times(a, block):
        return lax.dot_general(
            a.astype(jnp.bfloat16), block, (((1,), (1,)), ((), ())), preferred_element_type=jnp.float32
        )

    def blocks(body, init):
        def step(i, carry):
            return body(pl.ds(pl.multiple_of(i * BLOCK, BLOCK), BLOCK), carry)

        return lax.fori_loop(0, width // BLOCK, step, init)

    zero = jnp.zeros((count, 128), jnp.float32)
    none = jnp.zeros((count, grads.shape[0]), jnp.float32)

    sent = gather(t, 0, lambda lane: firsts[lane].wait())
    for copy in loads:
        copy.wait()

    def first(at, carry):
        proj, square = carry
        d = t[:, at]
        return proj + times(d, g[:, at]), square + fold(d * d)

    proj, square = blocks(first, (none, zero))
    norm = across(square)
    back = proj.astype(jnp.bfloat16)

    def spread(at, carry):
        acc[:, at] = jnp.dot(back, g[:, at], preferred_element_type=jnp.float32)
        return carry

    blocks(spread, 0)
    sent += scatter(1)

    def ready(lane):
        at = pl.ds(pl.multiple_of(place[lane] * chunk, chunk), chunk)
        img[rows[lane], at] = acc[rows[lane], at]

    sent += gather(img, 2, ready)
    for copy in sent:
        copy.wait_send()

    def image(at):
        return img[:, at] * (1.0 / n_total) + damping * t[:, at]

    alpha = norm / across(blocks(lambda at, c: c + fold(t[:, at] * image(at)), zero))

    def shrink(at, carry):
        r = t[:, at] - alpha * image(at)
        img[:, at] = r
        return carry + fold(r * r)

    after = across(blocks(shrink, zero))
    beta = after / norm

    def second(at, carry):
        proj, square = carry
        d = img[:, at] + beta * t[:, at]
        img[:, at] = d
        return proj + times(d, g[:, at]), square + fold(d * d)

    proj, square = blocks(second, (none, zero))
    curv = jnp.broadcast_to(across(proj * proj.astype(jnp.bfloat16).astype(jnp.float32)), (count, 128))
    sent = []
    for k, stage in enumerate(orders[0]):
        mail[0, k] = curv
        copy = pltpu.make_async_remote_copy(
            src_ref=mail.at[0, k],
            dst_ref=mail.at[1, k],
            send_sem=csend.at[k],
            recv_sem=crecv.at[k],
            device_id=partner(stage),
            device_id_type=MESH,
        )
        copy.start()
        copy.wait()
        curv = curv + mail[1, k]
    step = after / (curv[:, :1] * (1.0 / n_total) + damping * across(square))

    def last(at, total):
        x = alpha * t[:, at] + step * img[:, at]
        acc[:, at] = x
        return total + times(x, g[:, at])

    scores[...] = blocks(last, none) * width ** (-0.5)
    z = 0
    for stage in low:
        z = z * 2 + bit(stage)
    for s in range(nr):
        out[:, pl.ds(s * chunk, chunk)] = acc[:, pl.ds(pl.multiple_of((s * nc + z) * chunk, chunk), chunk)]


def per_device(nr, nc, grads, tests):
    n = nr * nc
    count, own = tests.shape
    held, width = grads.shape
    stages = bits_of(n)
    if n != 2**stages or nr < 2 or width % (128 * n) or width % BLOCK or count % (8 * LANES):
        return plain(grads, tests)
    whole = pltpu.VMEM((count, width), jnp.float32)
    return pl.pallas_call(
        functools.partial(kernel, nr, nc),
        out_shape=(
            jax.ShapeDtypeStruct((count, own), jnp.float32),
            jax.ShapeDtypeStruct((count, held), jnp.float32),
        ),
        in_specs=[pl.BlockSpec(memory_space=pl.ANY)] * 2,
        out_specs=[pl.BlockSpec(memory_space=pltpu.VMEM)] * 2,
        scratch_shapes=[
            pltpu.VMEM((held, width), jnp.bfloat16),
            whole,
            whole,
            whole,
            whole,
            pltpu.VMEM((2, stages, count, 128), jnp.float32),
            pltpu.SemaphoreType.DMA((n,)),
            pltpu.SemaphoreType.DMA((LANES,)),
            pltpu.SemaphoreType.DMA((3, LANES, stages)),
            pltpu.SemaphoreType.DMA((3, LANES, stages)),
            pltpu.SemaphoreType.DMA((stages,)),
            pltpu.SemaphoreType.DMA((stages,)),
        ],
        compiler_params=pltpu.CompilerParams(
            collective_id=0, has_side_effects=True, vmem_limit_bytes=48 * 2**20
        ),
    )(grads, tests)


def solution(mesh):
    placed = (P(("rows", "cols"), None), P(None, "cols"))
    return jax.shard_map(
        functools.partial(per_device, mesh.shape["rows"], mesh.shape["cols"]),
        mesh=mesh,
        in_specs=placed,
        out_specs=(P(None, "cols"), P(None, ("rows", "cols"))),
        check_vma=False,
    )
```

```python
import functools

import jax
import jax.numpy as jnp
from jax import lax
from jax.experimental import pallas as pl
from jax.experimental.pallas import tpu as pltpu
from jax.sharding import PartitionSpec as P

MESH = pl.DeviceIdType.MESH
LANES = 2
BLOCK = 1024

damping = 0.5


def plain(grads, tests):
    n_total = grads.shape[0] * lax.axis_size("rows") * lax.axis_size("cols")
    width = grads.shape[1]
    own = tests.shape[1]
    direction = lax.all_gather(tests, "cols", axis=1, tiled=True)
    norm_now = jnp.sum(direction * direction, axis=1)

    def project(d):
        return lax.dot_general(
            grads, d.astype(jnp.bfloat16), (((1,), (1,)), ((), ())), preferred_element_type=jnp.float32
        )

    partial_value = lax.dot_general(
        project(direction).astype(jnp.bfloat16), grads, (((0,), (0,)), ((), ())), preferred_element_type=jnp.float32
    )
    image = lax.psum(partial_value, ("rows", "cols")) / n_total + damping * direction
    alpha = norm_now / jnp.sum(direction * image, axis=1)
    solution = alpha[:, None] * direction
    residual = direction - alpha[:, None] * image
    norm_next = jnp.sum(residual * residual, axis=1)
    direction = residual + (norm_next / norm_now)[:, None] * direction
    proj = project(direction)
    curv = lax.psum(jnp.sum(proj * proj.astype(jnp.bfloat16).astype(jnp.float32), axis=0), ("rows", "cols"))
    curv = curv / n_total + damping * jnp.sum(direction * direction, axis=1)
    solution = solution + (norm_next / curv)[:, None] * direction
    scores = lax.dot_general(
        solution.astype(jnp.bfloat16), grads, (((1,), (1,)), ((), ())), preferred_element_type=jnp.float32
    )
    mine = lax.dynamic_slice_in_dim(solution, lax.axis_index("cols") * own, own, axis=1)
    return (mine, scores * width ** (-0.5))


def bits_of(count):
    return count.bit_length() - 1


def reverse_bits(value, count):
    out = 0
    for _ in range(count):
        out, value = out * 2 + value % 2, value // 2
    return out


def kernel(nr, nc, grads, tests, out, scores, g, t, acc, img, box, mail, load_sem, own_sem, send_sem, recv_sem, csend, crecv):
    me = {"rows": lax.axis_index("rows"), "cols": lax.axis_index("cols")}
    n = nr * nc
    count, own = tests.shape
    width = grads.shape[1]
    chunk = width // n
    n_total = grads.shape[0] * n
    span = count // LANES
    rest = list(range(1, bits_of(nr)))
    low = [("cols", b) for b in range(bits_of(nc))]
    core = [("rows", 0)]
    far = [("rows", b) for b in rest]
    orders = [core + far + low, core + far[::-1] + low]
    stages = len(orders[0])
    far = far + low
    turns = [core + far[k:3] + far[:k] + far[3:] for k in range(3)]

    def bit(stage):
        axis, b = stage
        return lax.rem(lax.div(me[axis], 2**b), 2)

    def partner(stage):
        axis, b = stage
        return {axis: me[axis] + (1 - 2 * bit(stage)) * 2**b}

    loads = []
    for v in range(n):
        at = reverse_bits(v % nc, bits_of(nc)) * nr + v // nc
        loads.append(
            pltpu.make_async_copy(
                grads.at[:, pl.ds(at * chunk, chunk)], g.at[:, pl.ds(v * chunk, chunk)], load_sem.at[v]
            )
        )
        loads[-1].start()

    def placed(order):
        v = 0
        for stage in order:
            v = v * 2 + bit(stage)
        return v

    lanes = [(pl.ds(lane * span, span), order, placed(order)) for lane, order in enumerate(orders)]
    turned = []
    at = 0
    for k, order in enumerate(turns):
        size = 8 * ((count // 8 + 2 - k) // 3)
        turned.append((pl.ds(at, size), order, placed(order)))
        at += size
    firsts = []
    for lane, (rows, order, v) in enumerate(lanes):
        copy = pltpu.make_async_copy(
            tests.at[rows, pl.ds(pl.multiple_of(lax.div(v, nc) * chunk, chunk), chunk)],
            t.at[rows, pl.ds(pl.multiple_of(v * chunk, chunk), chunk)],
            own_sem.at[lane],
        )
        copy.start()
        firsts.append(copy)

    barrier = pltpu.get_barrier_semaphore()
    for stage in orders[0]:
        pl.semaphore_signal(barrier, inc=1, device_id=partner(stage), device_id_type=MESH)
    pl.semaphore_wait(barrier, stages)

    def gather(buf, phase, lanes, ready):
        sent = []
        start = [v for _, _, v in lanes]
        flying = [None] * len(lanes)
        for k in range(stages):
            size = chunk * 2**k
            for lane, (rows, order, _) in enumerate(lanes):
                stage = order[stages - 1 - k]
                if k == 0:
                    ready(lane)
                else:
                    flying[lane].wait_recv()
                part = buf.at[rows, pl.ds(pl.multiple_of(start[lane] * chunk, size), size)]
                flying[lane] = pltpu.make_async_remote_copy(
                    src_ref=part,
                    dst_ref=part,
                    send_sem=send_sem.at[phase, lane, k],
                    recv_sem=recv_sem.at[phase, lane, k],
                    device_id=partner(stage),
                    device_id_type=MESH,
                )
                flying[lane].start()
                sent.append(flying[lane])
                start[lane] = start[lane] - bit(stage) * 2**k
        return sent, flying

    def scatter(phase, lanes, between):
        sent = []
        start = [0] * len(lanes)
        flying = [None] * len(lanes)
        offset = 0
        for k in range(stages + 1):
            half = width // 2 ** (k + 1)
            for lane, (rows, order, _) in enumerate(lanes):
                if k:
                    flying[lane].wait_recv()
                    at = pl.ds(pl.multiple_of(start[lane], 2 * half), 2 * half)
                    acc[rows, at] = acc[rows, at] + box[rows, pl.ds(offset - 2 * half, 2 * half)]
                if k < stages:
                    stage = order[k]
                    give = start[lane] + (1 - bit(stage)) * half
                    start[lane] = start[lane] + bit(stage) * half
                    flying[lane] = pltpu.make_async_remote_copy(
                        src_ref=acc.at[rows, pl.ds(pl.multiple_of(give, half), half)],
                        dst_ref=box.at[rows, pl.ds(offset, half)],
                        send_sem=send_sem.at[phase, lane, k],
                        recv_sem=recv_sem.at[phase, lane, k],
                        device_id=partner(stage),
                        device_id_type=MESH,
                    )
                    flying[lane].start()
                    sent.append(flying[lane])
            if k == 0:
                between()
            offset += half
        return sent

    def fold(x):
        total = x[:, :128]
        for i in range(1, x.shape[1] // 128):
            total = total + x[:, i * 128 : (i + 1) * 128]
        return total

    def across(x):
        return jnp.sum(x, axis=1, keepdims=True)

    def times(a, block):
        return lax.dot_general(
            a.astype(jnp.bfloat16), block, (((1,), (1,)), ((), ())), preferred_element_type=jnp.float32
        )

    def blocks(body, init, begin=0, size=width):
        def step(i, carry):
            return body(pl.ds(pl.multiple_of(begin + i * BLOCK, BLOCK), BLOCK), carry)

        return lax.fori_loop(0, size // BLOCK, step, init)

    half = width // 2
    mine = bit(core[0]) * half
    other = half - mine

    zero = jnp.zeros((count, 128), jnp.float32)
    none = jnp.zeros((count, grads.shape[0]), jnp.float32)

    sent, flying = gather(t, 0, lanes, lambda lane: firsts[lane].wait())
    for copy in loads:
        copy.wait()

    def first(at, carry):
        proj, square = carry
        d = t[:, at]
        return proj + times(d, g[:, at]), square + fold(d * d)

    carry = blocks(first, (none, zero), mine, half)
    for copy in flying:
        copy.wait_recv()
    proj, square = blocks(first, carry, other, half)
    norm = across(square)
    back = proj.astype(jnp.bfloat16)

    def spread(at, carry):
        acc[:, at] = jnp.dot(back, g[:, at], preferred_element_type=jnp.float32)
        return carry

    blocks(spread, 0, other, half)
    sent += scatter(1, turned, lambda: blocks(spread, 0, mine, half))

    def ready(lane):
        rows, _, v = turned[lane]
        at = pl.ds(pl.multiple_of(v * chunk, chunk), chunk)
        img[rows, at] = acc[rows, at]

    more, flying = gather(img, 2, turned, ready)

    def image(at):
        return img[:, at] * (1.0 / n_total) + damping * t[:, at]

    def inner(at, carry):
        return carry + fold(t[:, at] * image(at))

    carry = blocks(inner, zero, mine, half)
    for copy in flying:
        copy.wait_recv()
    alpha = norm / across(blocks(inner, carry, other, half))
    for copy in sent + more:
        copy.wait_send()

    def shrink(at, carry):
        r = t[:, at] - alpha * image(at)
        img[:, at] = r
        return carry + fold(r * r)

    after = across(blocks(shrink, zero))
    beta = after / norm

    def second(at, carry):
        proj, square = carry
        d = img[:, at] + beta * t[:, at]
        img[:, at] = d
        return proj + times(d, g[:, at]), square + fold(d * d)

    proj, square = blocks(second, (none, zero))
    curv = jnp.broadcast_to(across(proj * proj.astype(jnp.bfloat16).astype(jnp.float32)), (count, 128))
    sent = []
    for k, stage in enumerate(orders[0]):
        mail[0, k] = curv
        copy = pltpu.make_async_remote_copy(
            src_ref=mail.at[0, k],
            dst_ref=mail.at[1, k],
            send_sem=csend.at[k],
            recv_sem=crecv.at[k],
            device_id=partner(stage),
            device_id_type=MESH,
        )
        copy.start()
        copy.wait()
        curv = curv + mail[1, k]
    step = after / (curv[:, :1] * (1.0 / n_total) + damping * across(square))

    def last(at, total):
        x = alpha * t[:, at] + step * img[:, at]
        acc[:, at] = x
        return total + times(x, g[:, at])

    scores[...] = blocks(last, none) * width ** (-0.5)
    z = 0
    for stage in low:
        z = z * 2 + bit(stage)
    for s in range(nr):
        out[:, pl.ds(s * chunk, chunk)] = acc[:, pl.ds(pl.multiple_of((s * nc + z) * chunk, chunk), chunk)]


def per_device(nr, nc, grads, tests):
    n = nr * nc
    count, own = tests.shape
    held, width = grads.shape
    stages = bits_of(n)
    if n != 2**stages or width % (128 * n) or width % (2 * BLOCK) or count % (8 * LANES) or count < 24 or nr < 4 or nc < 2:
        return plain(grads, tests)
    whole = pltpu.VMEM((count, width), jnp.float32)
    return pl.pallas_call(
        functools.partial(kernel, nr, nc),
        out_shape=(
            jax.ShapeDtypeStruct((count, own), jnp.float32),
            jax.ShapeDtypeStruct((count, held), jnp.float32),
        ),
        in_specs=[pl.BlockSpec(memory_space=pl.ANY)] * 2,
        out_specs=[pl.BlockSpec(memory_space=pltpu.VMEM)] * 2,
        scratch_shapes=[
            pltpu.VMEM((held, width), jnp.bfloat16),
            whole,
            whole,
            whole,
            whole,
            pltpu.VMEM((2, stages, count, 128), jnp.float32),
            pltpu.SemaphoreType.DMA((n,)),
            pltpu.SemaphoreType.DMA((LANES,)),
            pltpu.SemaphoreType.DMA((3, 3, stages)),
            pltpu.SemaphoreType.DMA((3, 3, stages)),
            pltpu.SemaphoreType.DMA((stages,)),
            pltpu.SemaphoreType.DMA((stages,)),
        ],
        compiler_params=pltpu.CompilerParams(
            collective_id=0, has_side_effects=True, vmem_limit_bytes=48 * 2**20
        ),
    )(grads, tests)


def solution(mesh):
    placed = (P(("rows", "cols"), None), P(None, "cols"))
    return jax.shard_map(
        functools.partial(per_device, mesh.shape["rows"], mesh.shape["cols"]),
        mesh=mesh,
        in_specs=placed,
        out_specs=(P(None, "cols"), P(None, ("rows", "cols"))),
        check_vma=False,
    )
```

```python
import functools

import jax
import jax.numpy as jnp
from jax import lax
from jax.experimental import pallas as pl
from jax.experimental.pallas import tpu as pltpu
from jax.sharding import PartitionSpec as P

MESH = pl.DeviceIdType.MESH
LANES = 2
BLOCK = 1024

damping = 0.5


def plain(grads, tests):
    n_total = grads.shape[0] * lax.axis_size("rows") * lax.axis_size("cols")
    width = grads.shape[1]
    own = tests.shape[1]
    direction = lax.all_gather(tests, "cols", axis=1, tiled=True)
    norm_now = jnp.sum(direction * direction, axis=1)

    def project(d):
        return lax.dot_general(
            grads, d.astype(jnp.bfloat16), (((1,), (1,)), ((), ())), preferred_element_type=jnp.float32
        )

    partial_value = lax.dot_general(
        project(direction).astype(jnp.bfloat16), grads, (((0,), (0,)), ((), ())), preferred_element_type=jnp.float32
    )
    image = lax.psum(partial_value, ("rows", "cols")) / n_total + damping * direction
    alpha = norm_now / jnp.sum(direction * image, axis=1)
    solution = alpha[:, None] * direction
    residual = direction - alpha[:, None] * image
    norm_next = jnp.sum(residual * residual, axis=1)
    direction = residual + (norm_next / norm_now)[:, None] * direction
    proj = project(direction)
    curv = lax.psum(jnp.sum(proj * proj.astype(jnp.bfloat16).astype(jnp.float32), axis=0), ("rows", "cols"))
    curv = curv / n_total + damping * jnp.sum(direction * direction, axis=1)
    solution = solution + (norm_next / curv)[:, None] * direction
    scores = lax.dot_general(
        solution.astype(jnp.bfloat16), grads, (((1,), (1,)), ((), ())), preferred_element_type=jnp.float32
    )
    mine = lax.dynamic_slice_in_dim(solution, lax.axis_index("cols") * own, own, axis=1)
    return (mine, scores * width ** (-0.5))


def bits_of(count):
    return count.bit_length() - 1


def reverse_bits(value, count):
    out = 0
    for _ in range(count):
        out, value = out * 2 + value % 2, value // 2
    return out


def kernel(nr, nc, grads, tests, out, scores, g, t, acc, img, box, mail, load_sem, own_sem, send_sem, recv_sem, csend, crecv):
    me = {"rows": lax.axis_index("rows"), "cols": lax.axis_index("cols")}
    n = nr * nc
    count, own = tests.shape
    width = grads.shape[1]
    chunk = width // n
    n_total = grads.shape[0] * n
    span = count // LANES
    rest = list(range(1, bits_of(nr)))
    low = [("cols", b) for b in range(bits_of(nc))]
    core = [("rows", 0)]
    far = [("rows", b) for b in rest]
    orders = [core + far + low, core + far[::-1] + low]
    stages = len(orders[0])
    far = far + low
    turns = [core + far[k:3] + far[:k] + far[3:] for k in range(3)]

    def bit(stage):
        axis, b = stage
        return lax.rem(lax.div(me[axis], 2**b), 2)

    def partner(stage):
        axis, b = stage
        return {axis: me[axis] + (1 - 2 * bit(stage)) * 2**b}

    loads = []
    for v in range(n):
        at = reverse_bits(v % nc, bits_of(nc)) * nr + v // nc
        loads.append(
            pltpu.make_async_copy(
                grads.at[:, pl.ds(at * chunk, chunk)], g.at[:, pl.ds(v * chunk, chunk)], load_sem.at[v]
            )
        )
        loads[-1].start()

    def placed(order):
        v = 0
        for stage in order:
            v = v * 2 + bit(stage)
        return v

    lanes = [(pl.ds(lane * span, span), order, placed(order)) for lane, order in enumerate(orders)]
    turned = []
    at = 0
    for k, order in enumerate(turns):
        size = 8 * ((count // 8 + 2 - k) // 3)
        turned.append((pl.ds(at, size), order, placed(order)))
        at += size
    firsts = []
    for lane, (rows, order, v) in enumerate(lanes):
        copy = pltpu.make_async_copy(
            tests.at[rows, pl.ds(pl.multiple_of(lax.div(v, nc) * chunk, chunk), chunk)],
            t.at[rows, pl.ds(pl.multiple_of(v * chunk, chunk), chunk)],
            own_sem.at[lane],
        )
        copy.start()
        firsts.append(copy)

    barrier = pltpu.get_barrier_semaphore()
    row, col = me["rows"], me["cols"]
    groups = [
        (2, lax.rem(row, 2), lambda p: {"rows": row - lax.rem(row, 2) + p}),
        (nr // 2, lax.div(row, 2), lambda p: {"rows": p * 2 + lax.rem(row, 2)}),
        (nc, col, lambda p: {"cols": p}),
    ]
    greeted = 0
    for m, digit, device in groups:
        for d in range(1, m):
            pl.semaphore_signal(barrier, inc=1, device_id=device(lax.rem(digit + d, m)), device_id_type=MESH)
            greeted += 1
    pl.semaphore_wait(barrier, greeted)

    def gather(buf, phase, lanes, ready):
        sent = []
        start = [v for _, _, v in lanes]
        flying = [None] * len(lanes)
        for k in range(stages):
            size = chunk * 2**k
            for lane, (rows, order, _) in enumerate(lanes):
                stage = order[stages - 1 - k]
                if k == 0:
                    ready(lane)
                else:
                    flying[lane].wait_recv()
                part = buf.at[rows, pl.ds(pl.multiple_of(start[lane] * chunk, size), size)]
                flying[lane] = pltpu.make_async_remote_copy(
                    src_ref=part,
                    dst_ref=part,
                    send_sem=send_sem.at[phase, lane, k],
                    recv_sem=recv_sem.at[phase, lane, k],
                    device_id=partner(stage),
                    device_id_type=MESH,
                )
                flying[lane].start()
                sent.append(flying[lane])
                start[lane] = start[lane] - bit(stage) * 2**k
        return sent, flying

    def scatter(phase, lanes, between):
        sent = []
        start = [0] * len(lanes)
        flying = [None] * len(lanes)
        offset = 0
        for k in range(stages + 1):
            half = width // 2 ** (k + 1)
            for lane, (rows, order, _) in enumerate(lanes):
                if k:
                    flying[lane].wait_recv()
                    at = pl.ds(pl.multiple_of(start[lane], 2 * half), 2 * half)
                    acc[rows, at] = acc[rows, at] + box[rows, pl.ds(offset - 2 * half, 2 * half)]
                if k < stages:
                    stage = order[k]
                    give = start[lane] + (1 - bit(stage)) * half
                    start[lane] = start[lane] + bit(stage) * half
                    flying[lane] = pltpu.make_async_remote_copy(
                        src_ref=acc.at[rows, pl.ds(pl.multiple_of(give, half), half)],
                        dst_ref=box.at[rows, pl.ds(offset, half)],
                        send_sem=send_sem.at[phase, lane, k],
                        recv_sem=recv_sem.at[phase, lane, k],
                        device_id=partner(stage),
                        device_id_type=MESH,
                    )
                    flying[lane].start()
                    sent.append(flying[lane])
            if k == 0:
                between()
            offset += half
        return sent

    def fold(x):
        total = x[:, :128]
        for i in range(1, x.shape[1] // 128):
            total = total + x[:, i * 128 : (i + 1) * 128]
        return total

    def across(x):
        return jnp.sum(x, axis=1, keepdims=True)

    def times(a, block):
        return lax.dot_general(
            a.astype(jnp.bfloat16), block, (((1,), (1,)), ((), ())), preferred_element_type=jnp.float32
        )

    def blocks(body, init, begin=0, size=width):
        def step(i, carry):
            return body(pl.ds(pl.multiple_of(begin + i * BLOCK, BLOCK), BLOCK), carry)

        return lax.fori_loop(0, size // BLOCK, step, init)

    half = width // 2
    mine = bit(core[0]) * half
    other = half - mine

    zero = jnp.zeros((count, 128), jnp.float32)
    none = jnp.zeros((count, grads.shape[0]), jnp.float32)

    sent, flying = gather(t, 0, lanes, lambda lane: firsts[lane].wait())
    for copy in loads:
        copy.wait()

    def first(at, carry):
        proj, square = carry
        d = t[:, at]
        return proj + times(d, g[:, at]), square + fold(d * d)

    carry = blocks(first, (none, zero), mine, half)
    for copy in flying:
        copy.wait_recv()
    proj, square = blocks(first, carry, other, half)
    norm = across(square)
    back = proj.astype(jnp.bfloat16)

    def spread(at, carry):
        acc[:, at] = jnp.dot(back, g[:, at], preferred_element_type=jnp.float32)
        return carry

    blocks(spread, 0, other, half)
    sent += scatter(1, turned, lambda: blocks(spread, 0, mine, half))

    def ready(lane):
        rows, _, v = turned[lane]
        at = pl.ds(pl.multiple_of(v * chunk, chunk), chunk)
        img[rows, at] = acc[rows, at]

    more, flying = gather(img, 2, turned, ready)

    def image(at):
        return img[:, at] * (1.0 / n_total) + damping * t[:, at]

    def inner(at, carry):
        return carry + fold(t[:, at] * image(at))

    carry = blocks(inner, zero, mine, half)
    for copy in flying:
        copy.wait_recv()
    alpha = norm / across(blocks(inner, carry, other, half))
    for copy in sent + more:
        copy.wait_send()

    def shrink(at, carry):
        r = t[:, at] - alpha * image(at)
        img[:, at] = r
        return carry + fold(r * r)

    after = across(blocks(shrink, zero))
    beta = after / norm

    def second(at, carry):
        proj, square = carry
        d = img[:, at] + beta * t[:, at]
        img[:, at] = d
        return proj + times(d, g[:, at]), square + fold(d * d)

    proj, square = blocks(second, (none, zero))
    curv = jnp.broadcast_to(across(proj * proj.astype(jnp.bfloat16).astype(jnp.float32)), (count, 128))
    sent = []
    for k, (m, digit, device) in enumerate(groups):
        mail[k, digit] = curv
        flying = []
        for d in range(1, m):
            copy = pltpu.make_async_remote_copy(
                src_ref=mail.at[k, digit],
                dst_ref=mail.at[k, digit],
                send_sem=csend.at[k, d],
                recv_sem=crecv.at[k, d],
                device_id=device(lax.rem(digit + d, m)),
                device_id_type=MESH,
            )
            copy.start()
            flying.append(copy)
        for copy in flying:
            copy.wait_recv()
        sent += flying
        curv = mail[k, 0]
        for p in range(1, m):
            curv = curv + mail[k, p]
    for copy in sent:
        copy.wait_send()
    step = after / (curv[:, :1] * (1.0 / n_total) + damping * across(square))

    def last(at, total):
        x = alpha * t[:, at] + step * img[:, at]
        acc[:, at] = x
        return total + times(x, g[:, at])

    scores[...] = blocks(last, none) * width ** (-0.5)
    z = 0
    for stage in low:
        z = z * 2 + bit(stage)
    for s in range(nr):
        out[:, pl.ds(s * chunk, chunk)] = acc[:, pl.ds(pl.multiple_of((s * nc + z) * chunk, chunk), chunk)]


def per_device(nr, nc, grads, tests):
    n = nr * nc
    count, own = tests.shape
    held, width = grads.shape
    stages = bits_of(n)
    widest = max(nr // 2, nc)
    if n != 2**stages or width % (128 * n) or width % (2 * BLOCK) or count % (8 * LANES) or count < 24 or nr < 4 or nc < 2:
        return plain(grads, tests)
    whole = pltpu.VMEM((count, width), jnp.float32)
    return pl.pallas_call(
        functools.partial(kernel, nr, nc),
        out_shape=(
            jax.ShapeDtypeStruct((count, own), jnp.float32),
            jax.ShapeDtypeStruct((count, held), jnp.float32),
        ),
        in_specs=[pl.BlockSpec(memory_space=pl.ANY)] * 2,
        out_specs=[pl.BlockSpec(memory_space=pltpu.VMEM)] * 2,
        scratch_shapes=[
            pltpu.VMEM((held, width), jnp.bfloat16),
            whole,
            whole,
            whole,
            whole,
            pltpu.VMEM((3, widest, count, 128), jnp.float32),
            pltpu.SemaphoreType.DMA((n,)),
            pltpu.SemaphoreType.DMA((LANES,)),
            pltpu.SemaphoreType.DMA((3, 3, stages)),
            pltpu.SemaphoreType.DMA((3, 3, stages)),
            pltpu.SemaphoreType.DMA((3, widest)),
            pltpu.SemaphoreType.DMA((3, widest)),
        ],
        compiler_params=pltpu.CompilerParams(
            collective_id=0, has_side_effects=True, vmem_limit_bytes=48 * 2**20
        ),
    )(grads, tests)


def solution(mesh):
    placed = (P(("rows", "cols"), None), P(None, "cols"))
    return jax.shard_map(
        functools.partial(per_device, mesh.shape["rows"], mesh.shape["cols"]),
        mesh=mesh,
        in_specs=placed,
        out_specs=(P(None, "cols"), P(None, ("rows", "cols"))),
        check_vma=False,
    )
```

```python
import functools

import jax
import jax.numpy as jnp
from jax import lax
from jax.experimental import pallas as pl
from jax.experimental.pallas import tpu as pltpu
from jax.sharding import PartitionSpec as P

MESH = pl.DeviceIdType.MESH
LANES = 2
BLOCK = 1024

damping = 0.5


def plain(grads, tests):
    n_total = grads.shape[0] * lax.axis_size("rows") * lax.axis_size("cols")
    width = grads.shape[1]
    own = tests.shape[1]
    direction = lax.all_gather(tests, "cols", axis=1, tiled=True)
    norm_now = jnp.sum(direction * direction, axis=1)

    def project(d):
        return lax.dot_general(
            grads, d.astype(jnp.bfloat16), (((1,), (1,)), ((), ())), preferred_element_type=jnp.float32
        )

    partial_value = lax.dot_general(
        project(direction).astype(jnp.bfloat16), grads, (((0,), (0,)), ((), ())), preferred_element_type=jnp.float32
    )
    image = lax.psum(partial_value, ("rows", "cols")) / n_total + damping * direction
    alpha = norm_now / jnp.sum(direction * image, axis=1)
    solution = alpha[:, None] * direction
    residual = direction - alpha[:, None] * image
    norm_next = jnp.sum(residual * residual, axis=1)
    direction = residual + (norm_next / norm_now)[:, None] * direction
    proj = project(direction)
    curv = lax.psum(jnp.sum(proj * proj.astype(jnp.bfloat16).astype(jnp.float32), axis=0), ("rows", "cols"))
    curv = curv / n_total + damping * jnp.sum(direction * direction, axis=1)
    solution = solution + (norm_next / curv)[:, None] * direction
    scores = lax.dot_general(
        solution.astype(jnp.bfloat16), grads, (((1,), (1,)), ((), ())), preferred_element_type=jnp.float32
    )
    mine = lax.dynamic_slice_in_dim(solution, lax.axis_index("cols") * own, own, axis=1)
    return (mine, scores * width ** (-0.5))


def bits_of(count):
    return count.bit_length() - 1


def reverse_bits(value, count):
    out = 0
    for _ in range(count):
        out, value = out * 2 + value % 2, value // 2
    return out


def kernel(nr, nc, grads, tests, out, scores, g, t, acc, img, box, mail, load_sem, own_sem, send_sem, recv_sem, csend, crecv):
    me = {"rows": lax.axis_index("rows"), "cols": lax.axis_index("cols")}
    n = nr * nc
    count, own = tests.shape
    width = grads.shape[1]
    chunk = width // n
    n_total = grads.shape[0] * n
    span = count // LANES
    rest = list(range(1, bits_of(nr)))
    low = [("cols", b) for b in range(bits_of(nc))]
    core = [("rows", 0)]
    far = [("rows", b) for b in rest]
    orders = [core + far + low, core + far[::-1] + low]
    stages = len(orders[0])
    far = far + low
    turns = [core + far[k:3] + far[:k] + far[3:] for k in range(3)]

    def bit(stage):
        axis, b = stage
        return lax.rem(lax.div(me[axis], 2**b), 2)

    def partner(stage):
        axis, b = stage
        return {axis: me[axis] + (1 - 2 * bit(stage)) * 2**b}

    loads = []
    for v in range(n):
        at = reverse_bits(v % nc, bits_of(nc)) * nr + v // nc
        loads.append(
            pltpu.make_async_copy(
                grads.at[:, pl.ds(at * chunk, chunk)], g.at[:, pl.ds(v * chunk, chunk)], load_sem.at[v]
            )
        )
        loads[-1].start()

    def placed(order):
        v = 0
        for stage in order:
            v = v * 2 + bit(stage)
        return v

    lanes = [(pl.ds(lane * span, span), order, placed(order)) for lane, order in enumerate(orders)]
    turned = []
    at = 0
    for k, order in enumerate(turns):
        size = 8 * ((count // 8 + 2 - k) // 3)
        turned.append((pl.ds(at, size), order, placed(order)))
        at += size
    firsts = []
    for lane, (rows, order, v) in enumerate(lanes):
        copy = pltpu.make_async_copy(
            tests.at[rows, pl.ds(pl.multiple_of(lax.div(v, nc) * chunk, chunk), chunk)],
            t.at[rows, pl.ds(pl.multiple_of(v * chunk, chunk), chunk)],
            own_sem.at[lane],
        )
        copy.start()
        firsts.append(copy)

    barrier = pltpu.get_barrier_semaphore()
    row, col = me["rows"], me["cols"]
    groups = [
        (2, lax.rem(row, 2), lambda p: {"rows": row - lax.rem(row, 2) + p}),
        (nr // 2, lax.div(row, 2), lambda p: {"rows": p * 2 + lax.rem(row, 2)}),
        (nc, col, lambda p: {"cols": p}),
    ]
    greeted = 0
    for m, digit, device in groups:
        for d in range(1, m):
            pl.semaphore_signal(barrier, inc=1, device_id=device(lax.rem(digit + d, m)), device_id_type=MESH)
            greeted += 1
    pl.semaphore_wait(barrier, greeted)

    def gather(buf, phase, lanes, ready):
        sent = []
        start = [v for _, _, v in lanes]
        flying = [[] for _ in lanes]
        done = 0
        if phase == 0:
            done = bits_of(nc)
            for lane, (rows, _, v) in enumerate(lanes):
                ready(lane)
                part = buf.at[rows, pl.ds(pl.multiple_of(v * chunk, chunk), chunk)]
                for d in range(1, nc):
                    copy = pltpu.make_async_remote_copy(
                        src_ref=part,
                        dst_ref=part,
                        send_sem=send_sem.at[3, lane, d],
                        recv_sem=recv_sem.at[3, lane, d],
                        device_id={"cols": lax.rem(col + d, nc)},
                        device_id_type=MESH,
                    )
                    copy.start()
                    flying[lane].append(copy)
                    sent.append(copy)
                start[lane] = v - lax.rem(v, nc)
        for k in range(done, stages):
            size = chunk * 2**k
            for lane, (rows, order, _) in enumerate(lanes):
                stage = order[stages - 1 - k]
                if k == 0:
                    ready(lane)
                else:
                    for copy in flying[lane]:
                        copy.wait_recv()
                part = buf.at[rows, pl.ds(pl.multiple_of(start[lane] * chunk, size), size)]
                copy = pltpu.make_async_remote_copy(
                    src_ref=part,
                    dst_ref=part,
                    send_sem=send_sem.at[phase, lane, k],
                    recv_sem=recv_sem.at[phase, lane, k],
                    device_id=partner(stage),
                    device_id_type=MESH,
                )
                copy.start()
                flying[lane] = [copy]
                sent.append(copy)
                start[lane] = start[lane] - bit(stage) * 2**k
        return sent, [copy for copies in flying for copy in copies]

    def scatter(phase, lanes, between):
        sent = []
        start = [0] * len(lanes)
        flying = [None] * len(lanes)
        offset = 0
        for k in range(stages + 1):
            half = width // 2 ** (k + 1)
            for lane, (rows, order, _) in enumerate(lanes):
                if k:
                    flying[lane].wait_recv()
                    at = pl.ds(pl.multiple_of(start[lane], 2 * half), 2 * half)
                    acc[rows, at] = acc[rows, at] + box[rows, pl.ds(offset - 2 * half, 2 * half)]
                if k < stages:
                    stage = order[k]
                    give = start[lane] + (1 - bit(stage)) * half
                    start[lane] = start[lane] + bit(stage) * half
                    flying[lane] = pltpu.make_async_remote_copy(
                        src_ref=acc.at[rows, pl.ds(pl.multiple_of(give, half), half)],
                        dst_ref=box.at[rows, pl.ds(offset, half)],
                        send_sem=send_sem.at[phase, lane, k],
                        recv_sem=recv_sem.at[phase, lane, k],
                        device_id=partner(stage),
                        device_id_type=MESH,
                    )
                    flying[lane].start()
                    sent.append(flying[lane])
            if k == 0:
                between()
            offset += half
        return sent

    def fold(x):
        total = x[:, :128]
        for i in range(1, x.shape[1] // 128):
            total = total + x[:, i * 128 : (i + 1) * 128]
        return total

    def across(x):
        return jnp.sum(x, axis=1, keepdims=True)

    def times(a, block):
        return lax.dot_general(
            a.astype(jnp.bfloat16), block, (((1,), (1,)), ((), ())), preferred_element_type=jnp.float32
        )

    def blocks(body, init, begin=0, size=width):
        def step(i, carry):
            return body(pl.ds(pl.multiple_of(begin + i * BLOCK, BLOCK), BLOCK), carry)

        return lax.fori_loop(0, size // BLOCK, step, init)

    half = width // 2
    mine = bit(core[0]) * half
    other = half - mine

    zero = jnp.zeros((count, 128), jnp.float32)
    none = jnp.zeros((count, grads.shape[0]), jnp.float32)

    sent, flying = gather(t, 0, lanes, lambda lane: firsts[lane].wait())
    for copy in loads:
        copy.wait()

    def first(at, carry):
        proj, square = carry
        d = t[:, at]
        return proj + times(d, g[:, at]), square + fold(d * d)

    carry = blocks(first, (none, zero), mine, half)
    for copy in flying:
        copy.wait_recv()
    proj, square = blocks(first, carry, other, half)
    norm = across(square)
    back = proj.astype(jnp.bfloat16)

    def spread(at, carry):
        acc[:, at] = jnp.dot(back, g[:, at], preferred_element_type=jnp.float32)
        return carry

    blocks(spread, 0, other, half)
    sent += scatter(1, turned, lambda: blocks(spread, 0, mine, half))

    def ready(lane):
        rows, _, v = turned[lane]
        at = pl.ds(pl.multiple_of(v * chunk, chunk), chunk)
        img[rows, at] = acc[rows, at]

    more, flying = gather(img, 2, turned, ready)

    def image(at):
        return img[:, at] * (1.0 / n_total) + damping * t[:, at]

    def inner(at, carry):
        return carry + fold(t[:, at] * image(at))

    carry = blocks(inner, zero, mine, half)
    for copy in flying:
        copy.wait_recv()
    alpha = norm / across(blocks(inner, carry, other, half))
    for copy in sent + more:
        copy.wait_send()

    def shrink(at, carry):
        r = t[:, at] - alpha * image(at)
        img[:, at] = r
        return carry + fold(r * r)

    after = across(blocks(shrink, zero))
    beta = after / norm

    def second(at, carry):
        proj, square = carry
        d = img[:, at] + beta * t[:, at]
        img[:, at] = d
        return proj + times(d, g[:, at]), square + fold(d * d)

    proj, square = blocks(second, (none, zero))
    curv = jnp.broadcast_to(across(proj * proj.astype(jnp.bfloat16).astype(jnp.float32)), (count, 128))
    sent = []
    for k, (m, digit, device) in enumerate(groups):
        mail[k, digit] = curv
        flying = []
        for d in range(1, m):
            copy = pltpu.make_async_remote_copy(
                src_ref=mail.at[k, digit],
                dst_ref=mail.at[k, digit],
                send_sem=csend.at[k, d],
                recv_sem=crecv.at[k, d],
                device_id=device(lax.rem(digit + d, m)),
                device_id_type=MESH,
            )
            copy.start()
            flying.append(copy)
        for copy in flying:
            copy.wait_recv()
        sent += flying
        curv = mail[k, 0]
        for p in range(1, m):
            curv = curv + mail[k, p]
    for copy in sent:
        copy.wait_send()
    step = after / (curv[:, :1] * (1.0 / n_total) + damping * across(square))

    def last(at, total):
        x = alpha * t[:, at] + step * img[:, at]
        acc[:, at] = x
        return total + times(x, g[:, at])

    scores[...] = blocks(last, none) * width ** (-0.5)
    z = 0
    for stage in low:
        z = z * 2 + bit(stage)
    for s in range(nr):
        out[:, pl.ds(s * chunk, chunk)] = acc[:, pl.ds(pl.multiple_of((s * nc + z) * chunk, chunk), chunk)]


def per_device(nr, nc, grads, tests):
    n = nr * nc
    count, own = tests.shape
    held, width = grads.shape
    stages = bits_of(n)
    widest = max(nr // 2, nc)
    if n != 2**stages or width % (128 * n) or width % (2 * BLOCK) or count % (8 * LANES) or count < 24 or nr < 4 or nc < 2:
        return plain(grads, tests)
    whole = pltpu.VMEM((count, width), jnp.float32)
    return pl.pallas_call(
        functools.partial(kernel, nr, nc),
        out_shape=(
            jax.ShapeDtypeStruct((count, own), jnp.float32),
            jax.ShapeDtypeStruct((count, held), jnp.float32),
        ),
        in_specs=[pl.BlockSpec(memory_space=pl.ANY)] * 2,
        out_specs=[pl.BlockSpec(memory_space=pltpu.VMEM)] * 2,
        scratch_shapes=[
            pltpu.VMEM((held, width), jnp.bfloat16),
            whole,
            whole,
            whole,
            whole,
            pltpu.VMEM((3, widest, count, 128), jnp.float32),
            pltpu.SemaphoreType.DMA((n,)),
            pltpu.SemaphoreType.DMA((LANES,)),
            pltpu.SemaphoreType.DMA((4, 3, max(stages, nc))),
            pltpu.SemaphoreType.DMA((4, 3, max(stages, nc))),
            pltpu.SemaphoreType.DMA((3, widest)),
            pltpu.SemaphoreType.DMA((3, widest)),
        ],
        compiler_params=pltpu.CompilerParams(
            collective_id=0, has_side_effects=True, vmem_limit_bytes=48 * 2**20
        ),
    )(grads, tests)


def solution(mesh):
    placed = (P(("rows", "cols"), None), P(None, "cols"))
    return jax.shard_map(
        functools.partial(per_device, mesh.shape["rows"], mesh.shape["cols"]),
        mesh=mesh,
        in_specs=placed,
        out_specs=(P(None, "cols"), P(None, ("rows", "cols"))),
        check_vma=False,
    )
```
